32 devices in a mesh: dp: 2 (over x), tm: 2 (over y), space: 8 (over z, core).
Axes of the slice: x: 2, y: 2, z: 4, core: 2. Of those that a mesh axis runs over, the one named last changes fastest.
Arguments:
- latents: bfloat16 [32, 4, 128, 512], P(('dp', 'tm', 'space')), parts along dimension 0, may hold values from -36 to 36, as said below
- norm_gain: float32 [512], replicated, may hold values from 0.1 to 1.9
- conv_weight: bfloat16 [3, 3, 3, 512, 256], replicated, may hold values from -0.0546875 to 0.0546875
- skip_weight: bfloat16 [512, 256], replicated, may hold values from -0.25 to 0.25
- cotangent: bfloat16 [32, 8, 4, 16, 256], P(('dp', 'tm'), 'space'), parts along dimension 0, may hold values from -6 to 6
Outputs:
- output: bfloat16 [32, 8, 4, 16, 256], P(('dp', 'tm'), 'space'), parts along dimension 0
- grad_input: bfloat16 [32, 8, 4, 16, 512], P(('dp', 'tm'), 'space'), parts along dimension 0
The draws below stay inside these ranges and needn't reach their ends.
There are 2 independent parts, one for each index of `dp`. The reference program is written for one: setup_inputs(seed, part) draws one part's arguments, and reference() takes and returns one part's arrays. A program takes and returns all parts, laid end to end along the dimension named above; an argument that names none is the same for every part. Nothing has to cross between parts.
Inputs may be any that keep to these rules, and one draw needn't show every extreme that they name: `latents`: each cell and each channel has its own scale.
All inputs are finite; a program needn't handle non-finite values.
Results may differ from the reference program's by a relative error of at most 0.002.
Values may be sent and summed in bfloat16 or wider, within the bound.
No kernel may reach another device: no remote copies, remote signals or barrier semaphores. Data moves between devices by JAX's collectives and lax.ppermute only.
A program may use at most 192 MiB of HBM per device.

```python
import math
import jax
import jax.numpy as jnp
from jax import lax

C_IN = 512
C_OUT = 256
HEIGHT = 4
TW = 16
WIDTH = 128
FRAMES = 16
TILES = 8
N_SPACE = 8


def draw_latents(key, part):
    first, second, third = jax.random.split(key, 3)
    shape = (FRAMES, HEIGHT, WIDTH, C_IN)
    cell_scale = jnp.exp(jax.random.uniform(second, (FRAMES, HEIGHT, WIDTH, 1), jnp.float32, math.log(0.3), math.log(3.0)))
    chan_scale = jnp.exp(jax.random.uniform(third, (C_IN,), jnp.float32, math.log(0.3), math.log(3.0)))
    base = jnp.clip(jax.random.normal(first, shape, jnp.float32), -4.0, 4.0)
    return (base * cell_scale * chan_scale).astype(jnp.bfloat16)


def block_levels(stream_key, shape, cuts, low, top_value):
    gain, own = 1.0, jax.random.fold_in(stream_key, 6)
    for position, shards_of in cuts:
        steps = jnp.exp(jax.random.uniform(jax.random.fold_in(own, position), (shards_of,), jnp.float32, low / len(cuts), top_value / len(cuts)))
        gain = gain * jnp.repeat(steps, shape[position] // shards_of).reshape([-1 if axis == position else 1 for axis in range(len(shape))])
    return gain


def noise(own_key, extent, spread, bound, pieces=(), kind=jnp.bfloat16):
    loudness = block_levels(own_key, extent, pieces, -0.22, 0.18) if pieces else 1.0
    values = jax.random.normal(own_key, extent, jnp.float32) * spread * loudness
    return jnp.minimum(jnp.maximum(values, -bound), bound).astype(kind)


def setup_inputs(seed: int = 0, part: int = 0) -> dict:
    splits = jax.random.split(jax.random.key(seed), 6)
    part_keys = jax.random.split(jax.random.fold_in(splits[5], part), 6)
    return {
        "latents": draw_latents(jax.random.fold_in(jax.random.fold_in(splits[5], part), 71), part),
        "norm_gain": jnp.clip(1.0 + 0.18 * jax.random.normal(splits[1], (C_IN,), jnp.float32), 0.1, 1.9),
        "conv_weight": noise(splits[2], (3, 3, 3, C_IN, C_OUT), (27 * C_IN) ** -0.5, 0.0546875),
        "skip_weight": noise(splits[3], (C_IN, C_OUT), C_IN ** -0.5, 0.25),
        "cotangent": noise(part_keys[4], (FRAMES, TILES, HEIGHT, TW, C_OUT), 1.0, 6.0, ((0, 2), (1, 8))),
    }


epsilon = 1e-06

def activate(x_float, norm_gain):
    mean_sq = lax.optimization_barrier(jnp.mean(x_float * x_float, axis=-1, keepdims=True))
    inv_rms = lax.rsqrt(mean_sq + epsilon)
    unit_val = x_float * inv_rms
    return (inv_rms, unit_val, unit_val * norm_gain)

def silu_slope(normed):
    sigma_val = jax.nn.sigmoid(normed)
    return sigma_val * (1.0 + normed * (1.0 - sigma_val))

def to_tiles(whole, strips):
    frames, height, width, channels = whole.shape
    shaped = whole.reshape(frames, height, strips, width // strips, channels)
    return shaped.transpose(0, 2, 1, 3, 4)

def from_tiles(tiled):
    frames, count, height, tile_cols, channels = tiled.shape
    return tiled.transpose(0, 2, 1, 3, 4).reshape(frames, height, count * tile_cols, channels)

def reference(latents, norm_gain, conv_weight, skip_weight, cotangent):
    frames, height, width, in_chan = latents.shape
    out_chan = skip_weight.shape[1]
    x_float = latents.astype(jnp.float32)
    inv_rms, unit_val, normed = activate(x_float, norm_gain)
    hidden = jax.nn.silu(normed).astype(jnp.bfloat16)
    padded = jnp.pad(hidden, ((2, 0), (1, 1), (1, 1), (0, 0)))
    summed = jnp.dot(latents.reshape(-1, in_chan), skip_weight, preferred_element_type=jnp.float32)
    for t_tap in range(3):
        for h_tap in range(3):
            for w_tap in range(3):
                window = padded[t_tap:t_tap + frames, h_tap:h_tap + height, w_tap:w_tap + width]
                summed = summed + jnp.dot(window.reshape(-1, in_chan), conv_weight[t_tap, h_tap, w_tap], preferred_element_type=jnp.float32)
    output = summed.astype(jnp.bfloat16).reshape(frames, height, width, out_chan)
    grad_out = from_tiles(cotangent)
    grad_pad = jnp.pad(grad_out, ((0, 2), (1, 1), (1, 1), (0, 0)))
    grad_hidden = jnp.zeros((frames * height * width, in_chan), jnp.float32)
    for t_tap in range(3):
        for h_tap in range(3):
            for w_tap in range(3):
                window = grad_pad[2 - t_tap:2 - t_tap + frames, 2 - h_tap:2 - h_tap + height, 2 - w_tap:2 - w_tap + width]
                grad_hidden = grad_hidden + jnp.dot(window.reshape(-1, out_chan), conv_weight[t_tap, h_tap, w_tap].T, preferred_element_type=jnp.float32)
    grad_skip = jnp.dot(grad_out.reshape(-1, out_chan), skip_weight.T, preferred_element_type=jnp.float32)
    grad_unit = grad_hidden.reshape(frames, height, width, in_chan) * silu_slope(normed) * norm_gain
    grad_input = inv_rms * (grad_unit - unit_val * lax.optimization_barrier(jnp.mean(grad_unit * unit_val, axis=-1, keepdims=True)))
    grad_input = grad_input + grad_skip.reshape(frames, height, width, in_chan)
    return (to_tiles(output, N_SPACE), to_tiles(grad_input.astype(jnp.bfloat16), N_SPACE))
```

```python
import jax
import jax.numpy as jnp
from jax import lax
from jax.experimental import pallas as pl
from jax.experimental.pallas import tpu as pltpu
from jax.sharding import PartitionSpec as P

epsilon = 1e-06
f32 = jnp.float32
bf16 = jnp.bfloat16
vmem = pl.BlockSpec(memory_space=pltpu.VMEM)


def call(body, outs, ins, scratch=(), flops=0, moved=0, grant=24):
    return pl.pallas_call(
        body,
        out_shape=[jax.ShapeDtypeStruct(shape, dtype) for shape, dtype in outs],
        in_specs=[vmem] * len(ins),
        out_specs=[vmem] * len(outs),
        scratch_shapes=list(scratch),
        compiler_params=pltpu.CompilerParams(vmem_limit_bytes=grant << 20),
        cost_estimate=pl.CostEstimate(flops=flops, bytes_accessed=moved, transcendentals=0),
    )(*ins)


def iota(shape, dim):
    return lax.broadcasted_iota(jnp.int32, shape, dim)


def matmul(a, b, contract=(1, 0)):
    return lax.dot_general(
        a, b, (((contract[0],), (contract[1],)), ((), ())), preferred_element_type=f32
    )


def cut_body(strips, rows, width, cols, cells, lat, cot, *outs):
    slots, low, high = outs[:strips], outs[strips], outs[strips + 1]
    me = lax.axis_index("space")
    chans = lat.shape[-1]
    shape = (strips * 2 * rows, rows * width)
    line, cell = iota(shape, 0), iota(shape, 1)
    strip = jnp.bitwise_xor(lax.div(line, 2 * rows), me)
    side = lax.rem(lax.div(line, rows), 2)
    column = strip * cols + jnp.where(side == 0, -1, cols)
    target = jnp.where((column >= 0) & (column < width), lax.rem(line, rows) * width + column, -1)
    pick = jnp.where(cell == target, 1.0, 0.0).astype(bf16)
    rims = matmul(pick, lat[...].reshape(rows * width, chans)).astype(bf16)
    for k in range(strips):
        start = pl.multiple_of(jnp.bitwise_xor(me, k) * cols, cols)
        for h in range(rows):
            slots[k][h * cols : (h + 1) * cols, :] = lat[0, h, pl.ds(start, cols), :]
        slots[k][rows * cols :, :] = rims[k * 2 * rows : (k + 1) * 2 * rows]
    shape = (cells // cols, cells)
    spot = iota(shape, 1) - iota(shape, 0) * cols
    low[...] = matmul(jnp.where(spot == 0, 1.0, 0.0).astype(bf16), cot[...]).astype(bf16)
    high[...] = matmul(jnp.where(spot == cols - 1, 1.0, 0.0).astype(bf16), cot[...]).astype(bf16)


def three(value, left, right, cols):
    count, chans = value.shape
    rows = count // cols
    spot = lax.rem(iota((count, chans), 0), cols)

    def spread(rim):
        return jnp.concatenate(
            [jnp.broadcast_to(rim[r : r + 1], (cols, chans)) for r in range(rows)], 0
        )

    before = jnp.where(spot == 0, spread(left), pltpu.roll(value, 1, 0))
    after = jnp.where(spot == cols - 1, spread(right), pltpu.roll(value, count - 1, 0))
    return before, after


def put_three(ref, f, value, left, right, cols):
    rows = value.shape[0] // cols
    chans = value.shape[1]
    before, after = three(value, left, right, cols)
    for place, part in enumerate((before, value, after)):
        ref[f, :, :, place * chans : (place + 1) * chans] = part.astype(bf16).reshape(
            rows, cols, chans
        )


def grad_body(frames, rows, cols, cot, low, high, nxt, weight, skip, grad, direct, held):
    tile = rows * cols
    chans = cot.shape[-1]
    for f in range(frames):
        put_three(
            held,
            f,
            cot[f * tile : (f + 1) * tile, :].astype(f32),
            low[f * rows : (f + 1) * rows, :].astype(f32),
            high[f * rows : (f + 1) * rows, :].astype(f32),
            cols,
        )
    for f in range(2):
        rims = nxt[2 * tile + f * 2 * rows : 2 * tile + (f + 1) * 2 * rows, :].astype(f32)
        put_three(
            held,
            frames + f,
            nxt[f * tile : (f + 1) * tile, :].astype(f32),
            rims[:rows],
            rims[rows:],
            cols,
        )
    direct[...] = matmul(cot[...], skip[...], (1, 1))
    in_chan = grad.shape[-1]
    first = True
    for h_tap in (1, 0, 2):
        top, end = max(0, h_tap - 1), rows + min(0, h_tap - 1)
        for t_tap in range(3):
            window = held[
                2 - t_tap : 2 - t_tap + frames, top + 1 - h_tap : end + 1 - h_tap
            ].reshape(frames * (end - top) * cols, 3 * chans)
            side = jnp.concatenate([weight[t_tap, h_tap, 2 - c] for c in range(3)], axis=1)
            part = matmul(window, side, (1, 1)).reshape(frames, end - top, cols, in_chan)
            if first:
                grad[:, top:end] = part
                first = False
            else:
                grad[:, top:end] += part


def normed_parts(x, gain):
    mean_sq = jnp.mean(x * x, axis=-1, keepdims=True)
    inv_rms = lax.rsqrt(mean_sq + epsilon)
    unit_val = x * inv_rms
    normed = unit_val * gain
    sigma_val = 0.5 * jnp.tanh(0.5 * normed) + 0.5
    return inv_rms, unit_val, normed, sigma_val


def last_body(strips, frames, tile, gain, after, *refs):
    slots, out = refs[:strips], refs[strips]
    held = refs[strips + 1]
    me = lax.axis_index("space")
    extra = slots[0].shape[0] - tile
    for k in range(strips):
        frame = jnp.bitwise_xor(me, k)

        @pl.when(frame >= frames - 2)
        def _():
            held[frame - (frames - 2)] = slots[k][...]

    for f in range(2):
        _, _, normed, sigma_val = normed_parts(held[f].astype(f32), gain[...])
        hidden = (normed * sigma_val).astype(bf16)
        out[f * tile : (f + 1) * tile, :] = hidden[:tile]
        out[2 * tile + f * extra : 2 * tile + (f + 1) * extra, :] = hidden[tile:]


def here_body(strips, frames, rows, cols, gain, weight, skip, grad, direct, *refs):
    slots = refs[:strips]
    grad_in, held, total, tiles = refs[strips:]
    me = lax.axis_index("space")
    tile = rows * cols
    for k in range(strips):
        frame = jnp.bitwise_xor(me, k)
        x = slots[k][...].astype(f32)
        inv_rms, unit_val, normed, sigma_val = normed_parts(x, gain[...])
        hidden = normed * sigma_val
        put_three(
            held, frame, hidden[:tile], hidden[tile : tile + rows], hidden[tile + rows :], cols
        )
        tiles[frame] = slots[k][:tile, :]
        inv_rms, unit_val, normed, sigma_val, hidden = (
            part[:tile] for part in (inv_rms, unit_val, normed, sigma_val, hidden)
        )
        slope = sigma_val * (1.0 + normed * (1.0 - sigma_val))
        grad_hidden = grad[frame].reshape(tile, x.shape[-1])
        grad_unit = grad_hidden * slope * gain[...]
        value = inv_rms * (
            grad_unit - unit_val * jnp.mean(grad_unit * unit_val, axis=-1, keepdims=True)
        )
        value = value + direct[pl.ds(pl.multiple_of(frame * tile, tile), tile), :]
        grad_in[frame] = value.astype(bf16)
    total[...] = matmul(tiles[...].reshape(frames * tile, -1), skip[...]).reshape(total.shape)
    taps(held, weight, total, frames, rows, cols, 2)


def taps(held, weight, total, frames, rows, cols, t_tap):
    wide = held.shape[-1]
    out_chan = total.shape[-1]
    for h_tap in (1, 0, 2):
        top, end = max(0, 1 - h_tap), rows + min(0, 1 - h_tap)
        window = held[:, top + h_tap - 1 : end + h_tap - 1].reshape(-1, wide)
        side = weight[t_tap, h_tap].reshape(wide, out_chan)
        total[:, top:end] += matmul(window, side).reshape(frames, end - top, cols, out_chan)


def past_body(frames, rows, cols, weight, held, total, past, out, work):
    tile = rows * cols
    chans = past.shape[-1]
    before = work
    for f in range(2):
        rims = past[2 * tile + f * 2 * rows : 2 * tile + (f + 1) * 2 * rows, :].astype(f32)
        put_three(
            before, f, past[f * tile : (f + 1) * tile, :].astype(f32), rims[:rows], rims[rows:], cols
        )
    out_chan = total.shape[-1]
    wide = 3 * chans
    acc = {}
    for h_tap in (1, 0, 2):
        top, end = max(0, 1 - h_tap), rows + min(0, 1 - h_tap)
        for t_tap in range(2):
            window = jnp.concatenate(
                [
                    before[t_tap:, top + h_tap - 1 : end + h_tap - 1],
                    held[: frames - 2 + t_tap, top + h_tap - 1 : end + h_tap - 1],
                ],
                0,
            ).reshape(frames * (end - top) * cols, wide)
            side = weight[t_tap, h_tap].reshape(wide, out_chan)
            total[:, top:end] += matmul(window, side).reshape(frames, end - top, cols, out_chan)
    out[...] = total[...].astype(bf16)


def local(latents, norm_gain, conv_weight, skip_weight, cotangent):
    strips = lax.axis_size("space")
    blocks = lax.axis_size("tm")
    frame_count, rows, width, in_chan = latents.shape
    frames, single, tile_rows, cols, out_chan = cotangent.shape
    assert frame_count == 1 and frames == strips and strips & (strips - 1) == 0
    tile = rows * cols
    cells = frames * tile
    extra = 2 * rows
    gain = norm_gain.reshape(1, in_chan)
    cot = cotangent.reshape(cells, out_chan)

    *slots, low, high = call(
        lambda *refs: cut_body(strips, rows, width, cols, cells, *refs),
        [((tile + extra, in_chan), bf16)] * strips + [((cells // cols, out_chan), bf16)] * 2,
        [latents, cot],
    )
    upward = [(i, i + 1) for i in range(strips - 1)]
    downward = [(b, a) for a, b in upward]
    arrived = {0: slots[0]}
    for k in range(1, strips // 2):
        arrived[k] = lax.ppermute(slots[k], "space", [(i, i ^ k) for i in range(strips)])
    from_low = lax.ppermute(high, "space", upward)
    from_high = lax.ppermute(low, "space", downward)
    for k in range(strips // 2, strips):
        arrived[k] = lax.ppermute(slots[k], "space", [(i, i ^ k) for i in range(strips)])
    arrived = [arrived[k] for k in range(strips)]

    rim = (2, rows, out_chan)
    rims = jnp.concatenate([from_low[: 2 * rows].reshape(rim), from_high[: 2 * rows].reshape(rim)], 1)
    own = jnp.concatenate([cot[: 2 * tile], rims.reshape(2 * extra, out_chan)], 0)
    nxt = lax.ppermute(own, "tm", [(i + 1, i) for i in range(blocks - 1)])

    grad, direct = call(
        lambda *refs: grad_body(frames, rows, cols, *refs),
        [((frames, rows, cols, in_chan), f32), ((cells, in_chan), f32)],
        [cot, from_low, from_high, nxt, conv_weight, skip_weight],
        [pltpu.VMEM((frames + 2, rows, cols, 3 * out_chan), bf16)],
        flops=2 * 27 * cells * in_chan * out_chan,
    )
    (last,) = call(
        lambda *refs: last_body(strips, frames, tile, *refs),
        [((2 * (tile + extra), in_chan), bf16)],
        [gain, direct, *arrived],
        [pltpu.VMEM((2, tile + extra, in_chan), bf16)],
    )
    past = lax.ppermute(last, "tm", [(i, i + 1) for i in range(blocks - 1)])
    grad_input, held, total = call(
        lambda *refs: here_body(strips, frames, rows, cols, *refs),
        [
            ((frames, tile, in_chan), bf16),
            ((frames, rows, cols, 3 * in_chan), bf16),
            ((frames, rows, cols, out_chan), f32),
        ],
        [gain, conv_weight, skip_weight, grad, direct, *arrived],
        [pltpu.VMEM((frames, tile, in_chan), bf16)],
        flops=2 * 9 * cells * in_chan * out_chan,
    )
    (output,) = call(
        lambda *refs: past_body(frames, rows, cols, *refs),
        [((frames, rows, cols, out_chan), bf16)],
        [conv_weight, held, total, past],
        [pltpu.VMEM((2, rows, cols, 3 * in_chan), bf16)],
        flops=2 * 18 * cells * in_chan * out_chan,
    )
    return (
        output.reshape(frames, 1, rows, cols, out_chan),
        grad_input.reshape(frames, 1, rows, cols, in_chan),
    )


def solution(mesh):
    placed = (
        P(("dp", "tm", "space"), None, None, None),
        P(),
        P(),
        P(),
        P(("dp", "tm"), "space", None, None, None),
    )
    return jax.shard_map(
        local,
        mesh=mesh,
        in_specs=placed,
        out_specs=(
            P(("dp", "tm"), "space", None, None, None),
            P(("dp", "tm"), "space", None, None, None),
        ),
        check_vma=False,
    )
```

```python
import jax
import jax.numpy as jnp
from jax import lax
from jax.experimental import pallas as pl
from jax.experimental.pallas import tpu as pltpu
from jax.sharding import PartitionSpec as P

epsilon = 1e-06
f32 = jnp.float32
bf16 = jnp.bfloat16
vmem = pl.BlockSpec(memory_space=pltpu.VMEM)
hbm = pl.BlockSpec(memory_space=pltpu.HBM)


def call(body, outs, ins, scratch=(), flops=0, moved=0, grant=24, specs=None, out_specs=None, aliases=None):
    return pl.pallas_call(
        body,
        out_shape=[jax.ShapeDtypeStruct(shape, dtype) for shape, dtype in outs],
        in_specs=specs or [vmem] * len(ins),
        out_specs=out_specs or [vmem] * len(outs),
        scratch_shapes=list(scratch),
        input_output_aliases=aliases or {},
        compiler_params=pltpu.CompilerParams(vmem_limit_bytes=grant << 20),
        cost_estimate=pl.CostEstimate(flops=flops, bytes_accessed=moved, transcendentals=0),
    )(*ins)


def iota(shape, dim):
    return lax.broadcasted_iota(jnp.int32, shape, dim)


def matmul(a, b, contract=(1, 0)):
    return lax.dot_general(
        a, b, (((contract[0],), (contract[1],)), ((), ())), preferred_element_type=f32
    )


def in_hbm(value):
    return pltpu.with_memory_space_constraint(value, pltpu.HBM)


def place():
    me = lax.axis_index("space")
    return lax.div(me, 2), lax.rem(me, 2)


def one_hot(hit):
    return jnp.where(hit, 1.0, 0.0).astype(bf16)


def fold(edge):
    half = edge.shape[0] // 2
    return jnp.concatenate([edge[:half], edge[half:]], 1)


def unfold(packed):
    half = packed.shape[1] // 2
    return jnp.concatenate([packed[:, :half], packed[:, half:]], 0)


def cut_body(dims, lat_hbm, cot_hbm, mine, theirs, cot, lat, sems):
    chips, rows, width, cols, cells = dims
    first = pltpu.make_async_copy(lat_hbm, lat, sems.at[0])
    second = pltpu.make_async_copy(cot_hbm, cot, sems.at[1])
    first.start()
    second.start()
    _, core = place()
    chans = lat.shape[-1]
    tile = rows * cols
    shape = (chips * 4 * rows, rows * width)
    line, cell = iota(shape, 0), iota(shape, 1)
    owner = jnp.bitwise_xor(core, lax.rem(lax.div(line, 2 * rows), 2))
    strip = 2 * lax.div(line, 4 * rows) + owner
    side = lax.rem(lax.div(line, rows), 2)
    column = strip * cols + jnp.where(side == 0, -1, cols)
    target = jnp.where((column >= 0) & (column < width), lax.rem(line, rows) * width + column, -1)
    pick = one_hot(cell == target)
    shape = (cells // cols, cells)
    spot = iota(shape, 1) - iota(shape, 0) * cols
    pick_low, pick_high = one_hot(spot == 0), one_hot(spot == cols - 1)
    first.wait()
    rims = matmul(pick, lat[...].reshape(rows * width, chans)).astype(bf16)
    for z in range(chips):
        for who, ref in enumerate((mine, theirs)):
            start = pl.multiple_of((2 * z + jnp.bitwise_xor(core, who)) * cols, cols)
            for h in range(rows):
                ref[z, h * cols : (h + 1) * cols, :] = lat[0, h, pl.ds(start, cols), :]
            base = (2 * z + who) * 2 * rows
            ref[z, tile : tile + 2 * rows, :] = rims[base : base + 2 * rows]
    second.wait()
    half = cells // cols // 2
    theirs[chips, :half, :] = fold(matmul(pick_low, cot[...]).astype(bf16))
    theirs[chips, half : 2 * half, :] = fold(matmul(pick_high, cot[...]).astype(bf16))


def mix_body(chips, half, mine, got, *outs):
    pairs, outer = outs[:chips], outs[chips]
    chip, core = place()
    for q in range(chips):
        other = jnp.bitwise_xor(chip, q)
        pairs[q][core] = mine[other]
        pairs[q][1 - core] = got[other]
    outer[...] = unfold(jnp.where(core == 0, got[chips, half : 2 * half, :], got[chips, :half, :]))


def edge_body(chips, half, tile, rows, cot, got, outer, left, right, own):
    chip, core = place()
    inner = unfold(jnp.where(core == 0, got[chips, :half, :], got[chips, half : 2 * half, :]))
    edge = chip == jnp.where(core == 0, 0, chips - 1)
    far = jnp.where(edge, jnp.zeros_like(inner), outer[...])
    low = jnp.where(core == 0, far, inner)
    high = jnp.where(core == 0, inner, far)
    left[...] = low
    right[...] = high
    own[: 2 * tile, :] = cot[: 2 * tile, :]
    for f in range(2):
        start = 2 * tile + f * 2 * rows
        part = slice(f * rows, (f + 1) * rows)
        own[start : start + 2 * rows, :] = jnp.concatenate(
            [low[part].astype(f32), high[part].astype(f32)], 0
        ).astype(bf16)


def rimmed_frame(ref, f, tile, rows, keep):
    start = 2 * tile + f * 2 * rows
    value = ref[f * tile : (f + 1) * tile, :].astype(f32)
    rims = ref[start : start + 2 * rows, :].astype(f32)
    value = jnp.where(keep, value, 0.0)
    rims = jnp.where(keep, rims, 0.0)
    return value, rims[:rows], rims[rows:]


def put_three(ref, f, value, left, right, cols):
    count, chans = value.shape
    rows = count // cols
    spot = lax.rem(iota((count, chans), 0), cols)

    def spread(rim):
        return jnp.concatenate(
            [jnp.broadcast_to(rim[r : r + 1], (cols, chans)) for r in range(rows)], 0
        )

    before = jnp.where(spot == 0, spread(left), pltpu.roll(value, 1, 0))
    after = jnp.where(spot == cols - 1, spread(right), pltpu.roll(value, count - 1, 0))
    for index, part in enumerate((before, value, after)):
        ref[f, :, :, index * chans : (index + 1) * chans] = part.astype(bf16).reshape(
            rows, cols, chans
        )


def grad_body(
    frames, rows, cols, cot, low, high, nxt, weight_hbm, skip_hbm, grad, direct, weight, skip, held, sems
):
    order = [(h_tap, t_tap) for h_tap in (1, 0, 2) for t_tap in range(3)]
    loads = [pltpu.make_async_copy(skip_hbm, skip, sems.at[len(order)])]
    for index, (h_tap, t_tap) in enumerate(order):
        loads.append(
            pltpu.make_async_copy(
                weight_hbm.at[t_tap, h_tap], weight.at[t_tap, h_tap], sems.at[index]
            )
        )
    ahead = 3
    for load in loads[:ahead]:
        load.start()
    tile = rows * cols
    chans = cot.shape[-1]
    for f in range(frames):
        put_three(
            held,
            f,
            cot[f * tile : (f + 1) * tile, :].astype(f32),
            low[f * rows : (f + 1) * rows, :].astype(f32),
            high[f * rows : (f + 1) * rows, :].astype(f32),
            cols,
        )
    keep = lax.axis_index("tm") < lax.axis_size("tm") - 1
    for f in range(2):
        put_three(held, frames + f, *rimmed_frame(nxt, f, tile, rows, keep), cols)
    loads[0].wait()
    direct[...] = matmul(cot[...], skip[...], (1, 1))
    in_chan = grad.shape[-1]
    for index, (h_tap, t_tap) in enumerate(order):
        if index + ahead < len(loads):
            loads[index + ahead].start()
        loads[index + 1].wait()
        top, end = max(0, h_tap - 1), rows + min(0, h_tap - 1)
        window = held[
            2 - t_tap : 2 - t_tap + frames, top + 1 - h_tap : end + 1 - h_tap
        ].reshape(frames * (end - top) * cols, 3 * chans)
        side = jnp.concatenate([weight[t_tap, h_tap, 2 - c] for c in range(3)], axis=1)
        part = matmul(window, side, (1, 1)).reshape(frames, end - top, cols, in_chan)
        if (h_tap, t_tap) == order[0]:
            grad[:, top:end] = part
        else:
            grad[:, top:end] += part


def normed_parts(x, gain):
    mean_sq = jnp.mean(x * x, axis=-1, keepdims=True)
    inv_rms = lax.rsqrt(mean_sq + epsilon)
    unit_val = x * inv_rms
    normed = unit_val * gain
    sigma_val = 0.5 * jnp.tanh(0.5 * normed) + 0.5
    return inv_rms, unit_val, normed, sigma_val


def last_body(chips, tile, gain, after, *refs):
    pairs, out, held = refs[:chips], refs[chips], refs[chips + 1]
    chip, _ = place()
    extra = pairs[0].shape[1] - tile
    for q in range(chips):

        @pl.when(jnp.bitwise_xor(chip, q) == chips - 1)
        def _():
            held[...] = pairs[q][...]

    for f in range(2):
        _, _, normed, sigma_val = normed_parts(held[f].astype(f32), gain[...])
        hidden = (normed * sigma_val).astype(bf16)
        out[f * tile : (f + 1) * tile, :] = hidden[:tile]
        out[2 * tile + f * extra : 2 * tile + (f + 1) * extra, :] = hidden[tile:]


def frame_work(x, spot, frame, dims, gain, grad, direct, held, tiles, put):
    rows, cols = dims
    tile = rows * cols
    tiles[spot] = x[:tile]
    x = x.astype(f32)
    parts = normed_parts(x, gain[...])
    hidden = parts[2] * parts[3]
    put_three(held, spot, hidden[:tile], hidden[tile : tile + rows], hidden[tile + rows :], cols)
    inv_rms, unit_val, normed, sigma_val = (part[:tile] for part in parts)
    slope = sigma_val * (1.0 + normed * (1.0 - sigma_val))
    grad_unit = grad[frame].reshape(tile, x.shape[-1]) * slope * gain[...]
    value = inv_rms * (
        grad_unit - unit_val * jnp.mean(grad_unit * unit_val, axis=-1, keepdims=True)
    )
    value = value + direct[pl.ds(pl.multiple_of(frame * tile, tile), tile), :]
    put(value.astype(bf16))


def skip_product(base, dims, tiles, skip, total):
    rows, cols = dims
    total[pl.ds(base, 4)] += matmul(tiles[...].reshape(4 * rows * cols, -1), skip[...]).reshape(
        4, rows, cols, total.shape[-1]
    )


def group_taps(base, dims, held, weight, total):
    rows, cols = dims
    wide, out_chan = held.shape[-1], total.shape[-1]
    for h_tap in (1, 0, 2):
        top, end = max(0, 1 - h_tap), rows + min(0, 1 - h_tap)
        window = held[:, top + h_tap - 1 : end + h_tap - 1].reshape(-1, wide)
        for t_tap in (2, 1, 0):
            part = matmul(window, weight[t_tap, h_tap].reshape(wide, out_chan))
            total[pl.ds(base + 2 - t_tap, 4), top:end] += part.reshape(
                4, end - top, cols, out_chan
            )


def near_body(dims, gain, weight, skip, grad, direct, pair0, pair1, gis, total, held, tiles):
    chip, _ = place()
    base = 4 * lax.div(chip, 2)
    total[...] = jnp.zeros_like(total)
    for q, pair in enumerate((pair0, pair1)):
        for p in range(2):
            spot = 2 * jnp.bitwise_xor(lax.rem(chip, 2), q) + p

            def put(value):
                gis[spot] = value

            frame_work(pair[p], spot, base + spot, dims, gain, grad, direct, held, tiles, put)
    skip_product(base, dims, tiles, skip, total)
    group_taps(base, dims, held, weight, total)


def far_body(chips, dims, gain, weight, skip, grad, direct, gis, done, after, *refs):
    count = chips - 2
    pairs = refs[:count]
    grad_in, out, early, held, total, tiles, put_gi, put_out, sems = refs[count:]
    chip, _ = place()
    copies = [pltpu.make_async_copy(gis, grad_in.at[pl.ds(4 * lax.div(chip, 2), 4)], sems.at[0])]
    copies[0].start()
    total[...] = done[...]
    for m in range(1, chips // 2):
        base = 4 * jnp.bitwise_xor(lax.div(chip, 2), m)
        for q in (2 * m, 2 * m + 1):
            for p in range(2):
                spot = 2 * jnp.bitwise_xor(lax.rem(chip, 2), q % 2) + p

                def put(value):
                    put_gi[m - 1, spot] = value

                frame_work(
                    pairs[q - 2][p],
                    spot,
                    base + spot,
                    dims,
                    gain,
                    grad,
                    direct,
                    held,
                    tiles,
                    put,
                )
        copies.append(
            pltpu.make_async_copy(put_gi.at[m - 1], grad_in.at[pl.ds(base, 4)], sems.at[m])
        )
        copies[-1].start()
        skip_product(base, dims, tiles, skip, total)
        group_taps(base, dims, held, weight, total)
    early[...] = total[:2]
    put_out[...] = total[2 : put_out.shape[0] + 2].astype(bf16)
    copies.append(pltpu.make_async_copy(put_out, out.at[pl.ds(2, put_out.shape[0])], sems.at[chips // 2]))
    copies[-1].start()
    for copy in copies:
        copy.wait()


def past_body(dims, weight, done, past, whole, out, before, total, put, sem):
    rows, cols = dims
    wide, out_chan = before.shape[-1], done.shape[-1]
    keep = lax.axis_index("tm") > 0
    total[...] = done[...]
    for f in range(2):
        put_three(before, f, *rimmed_frame(past, f, rows * cols, rows, keep), cols)
    for h_tap in (1, 0, 2):
        top, end = max(0, 1 - h_tap), rows + min(0, 1 - h_tap)
        lines = slice(top + h_tap - 1, end + h_tap - 1)
        for t_tap in range(2):
            window = before[t_tap:, lines].reshape(-1, wide)
            part = matmul(window, weight[t_tap, h_tap].reshape(wide, out_chan))
            total[: 2 - t_tap, top:end] += part.reshape(2 - t_tap, end - top, cols, out_chan)
    put[...] = total[...].astype(bf16)
    copy = pltpu.make_async_copy(put, out.at[pl.ds(0, 2)], sem)
    copy.start()
    copy.wait()


def local(latents, norm_gain, conv_weight, skip_weight, cotangent):
    strips = lax.axis_size("space")
    blocks = lax.axis_size("tm")
    frame_count, rows, width, in_chan = latents.shape
    frames, _, _, cols, out_chan = cotangent.shape
    chips = strips // 2
    assert frame_count == 1 and frames == strips and chips & (chips - 1) == 0 and chips >= 4
    tile = rows * cols
    cells = frames * tile
    span = tile + 2 * rows
    half = cells // cols // 2
    dims = (rows, cols)
    gain = norm_gain.reshape(1, in_chan)
    cot = cotangent.reshape(cells, out_chan)
    strip = ((chips + 1, span, in_chan), bf16)
    pair = ((2, span, in_chan), bf16)

    mine, theirs, cot = call(
        lambda *refs: cut_body((chips, rows, width, cols, cells), *refs),
        [((chips, span, in_chan), bf16), strip, (cot.shape, bf16)],
        [in_hbm(latents), in_hbm(cot)],
        [pltpu.VMEM(latents.shape, bf16), pltpu.SemaphoreType.DMA((2,))],
        specs=[hbm, hbm],
    )
    got = lax.ppermute(theirs, "space", [(i, i ^ 1) for i in range(strips)])
    *pairs, outer = call(
        lambda *refs: mix_body(chips, half, *refs),
        [pair] * chips + [((2 * half, out_chan), bf16)],
        [mine, got],
    )
    for q in (*range(2, chips), 1):
        pairs[q] = lax.ppermute(pairs[q], "space", [(i, i ^ (2 * q)) for i in range(strips)])
    steps = {i: i + 2 - 4 * (i % 2) for i in range(strips)}
    steps[1], steps[strips - 2] = 0, strips - 1
    outer = lax.ppermute(outer, "space", list(steps.items()))
    left, right, own = call(
        lambda *refs: edge_body(chips, half, tile, rows, *refs),
        [((2 * half, out_chan), bf16)] * 2 + [((2 * span, out_chan), bf16)],
        [cot, got, outer],
    )
    nxt = lax.ppermute(own, "tm", [(i, (i - 1) % blocks) for i in range(blocks)])

    grad, direct, weight, skip = call(
        lambda *refs: grad_body(frames, rows, cols, *refs),
        [
            ((frames, rows, cols, in_chan), f32),
            ((cells, in_chan), f32),
            (conv_weight.shape, bf16),
            (skip_weight.shape, bf16),
        ],
        [cot, left, right, nxt, in_hbm(conv_weight), in_hbm(skip_weight)],
        [
            pltpu.VMEM((frames + 2, rows, cols, 3 * out_chan), bf16),
            pltpu.SemaphoreType.DMA((10,)),
        ],
        flops=2 * 27 * cells * in_chan * out_chan,
        specs=[vmem] * 4 + [hbm] * 2,
    )
    tiles = pltpu.VMEM((4, tile, in_chan), bf16)
    group = (4, rows, cols, 3 * in_chan)
    sums = ((frames + 2, rows, cols, out_chan), f32)
    gis, total = call(
        lambda *refs: near_body(dims, *refs),
        [((4, tile, in_chan), bf16), sums],
        [gain, weight, skip, grad, direct, pairs[0], pairs[1]],
        [pltpu.VMEM(group, bf16), tiles],
        flops=27 * cells * in_chan * out_chan,
    )
    (last,) = call(
        lambda *refs: last_body(chips, tile, *refs),
        [((2 * span, in_chan), bf16)],
        [gain, total, *pairs],
        [pltpu.VMEM((2, span, in_chan), bf16)],
    )
    past = lax.ppermute(last, "tm", [(i, (i + 1) % blocks) for i in range(blocks)])
    grad_input, output, total = call(
        lambda *refs: far_body(chips, dims, *refs),
        [
            ((frames, tile, in_chan), bf16),
            ((frames, rows, cols, out_chan), bf16),
            ((2, rows, cols, out_chan), f32),
        ],
        [gain, weight, skip, grad, direct, gis, total, last, *pairs[2:]],
        [
            pltpu.VMEM(group, bf16),
            pltpu.VMEM(*sums),
            tiles,
            pltpu.VMEM((chips // 2 - 1, 4, tile, in_chan), bf16),
            pltpu.VMEM((frames - 2, rows, cols, out_chan), bf16),
            pltpu.SemaphoreType.DMA((chips // 2 + 1,)),
        ],
        flops=27 * cells * in_chan * out_chan,
        out_specs=[hbm, hbm, vmem],
    )
    (output,) = call(
        lambda *refs: past_body(dims, *refs),
        [((frames, rows, cols, out_chan), bf16)],
        [weight, total, past, output],
        [
            pltpu.VMEM((2, *group[1:]), bf16),
            pltpu.VMEM((2, rows, cols, out_chan), f32),
            pltpu.VMEM((2, rows, cols, out_chan), bf16),
            pltpu.SemaphoreType.DMA,
        ],
        flops=4 * 27 * tile * in_chan * out_chan,
        specs=[vmem] * 3 + [hbm],
        out_specs=[hbm],
        aliases={3: 0},
    )
    return (
        output.reshape(frames, 1, rows, cols, out_chan),
        grad_input.reshape(frames, 1, rows, cols, in_chan),
    )


def solution(mesh):
    placed = (
        P(("dp", "tm", "space"), None, None, None),
        P(),
        P(),
        P(),
        P(("dp", "tm"), "space", None, None, None),
    )
    return jax.shard_map(
        local,
        mesh=mesh,
        in_specs=placed,
        out_specs=(
            P(("dp", "tm"), "space", None, None, None),
            P(("dp", "tm"), "space", None, None, None),
        ),
        check_vma=False,
    )
```
